32 devices in a mesh: seq: 32 (over z, y, x, core).
Axes of the slice: x: 2, y: 2, z: 4, core: 2. Of those that a mesh axis runs over, the one named last changes fastest.
Arguments:
- tokens: bfloat16 [65536, 320], P('seq'), may hold values from -6 to 6
- w_in: bfloat16 [2, 320, 640], replicated, may hold values from -0.3125 to 0.3125
- b_in: float32 [2, 640], replicated, may hold values from -3 to 3
- w_out: bfloat16 [2, 640, 320], replicated, may hold values from -0.25 to 0.25
- b_out: float32 [2, 320], replicated, may hold values from -3 to 3
- cotangent: bfloat16 [65536, 320], P('seq'), may hold values from -6 to 6
Outputs:
- result: bfloat16 [65536, 320], P('seq')
- grad_tokens: bfloat16 [65536, 320], P('seq')
- grad_w_in: float32 [2, 320, 640], replicated
- grad_b_in: float32 [2, 640], replicated
- grad_w_out: float32 [2, 640, 320], replicated
- grad_b_out: float32 [2, 320], replicated
The draws below stay inside these ranges and needn't reach their ends.
All inputs are finite; a program needn't handle non-finite values.
Results may differ from the reference program's by a relative error of at most 0.0065.
Values may be sent and summed in bfloat16 or wider, within the bound.
A program may use at most 128 MiB of HBM per device.

```python
import jax
import jax.numpy as jnp
from jax import lax

TRACKS = 20
TRACK_W = 16
D = 320
H = 640
LAYERS = 2
TOKENS = 65536


def shard_levels(key, extent, cuts, smallest, high):
    level, own = 1.0, jax.random.fold_in(key, 6)
    for position, shards_of in cuts:
        steps = jnp.exp(jax.random.uniform(jax.random.fold_in(own, position), (shards_of,), jnp.float32, smallest / len(cuts), high / len(cuts)))
        level = level * jnp.repeat(steps, extent[position] // shards_of).reshape([-1 if axis == position else 1 for axis in range(len(extent))])
    return level


def scatter_about(rng, extent, deviation, limit, cuts=(), kind=jnp.bfloat16):
    values = deviation * jax.random.normal(rng, extent, jnp.float32)
    if cuts:
        values = values * shard_levels(rng, extent, cuts, -0.22, 0.18)
    return jnp.clip(values, -limit, limit).astype(kind)


def setup_inputs(seed: int = 0) -> dict:
    streams_of = jax.random.split(jax.random.key(seed), 7)
    tokens = scatter_about(streams_of[0], (TOKENS, D), 1.0, 6.0, ((0, 32),))
    w_in = scatter_about(streams_of[1], (LAYERS, D, H), D ** -0.5, 0.3125)
    b_in = scatter_about(streams_of[2], (LAYERS, H), 0.5, 3.0, (), jnp.float32)
    w_out = scatter_about(streams_of[3], (LAYERS, H, D), H ** -0.5, 0.25)
    b_out = scatter_about(streams_of[4], (LAYERS, D), 0.5, 3.0, (), jnp.float32)
    cotangent = scatter_about(streams_of[5], (TOKENS, D), 1.0, 6.0, ((0, 32),))
    return {"tokens": tokens, "w_in": w_in, "b_in": b_in, "w_out": w_out, "b_out": b_out, "cotangent": cotangent}


def shift_of(track):
    if track == 0:
        return 0
    return min(2 ** (track - 1), TOKENS // 2)

def rotate(values, sign):
    pieces = []
    for track in range(TRACKS):
        block = values[:, track * TRACK_W:(track + 1) * TRACK_W]
        pieces.append(jnp.roll(block, sign * shift_of(track), axis=0))
    return jnp.concatenate(pieces, axis=1)

def gelu_tanh(t):
    return jax.nn.gelu(t, approximate=True)

def contract_rows(left, right):
    return lax.dot_general(left, right, (((0,), (0,)), ((), ())), preferred_element_type=jnp.float32)

def contract_cols(left, right):
    return lax.dot_general(left, right, (((1,), (1,)), ((), ())), preferred_element_type=jnp.float32)

def reference(tokens, w_in, b_in, w_out, b_out, cotangent):
    inputs = []
    current = tokens
    for layer in range(LAYERS):
        inputs.append(current)
        pre = jnp.dot(current, w_in[layer], preferred_element_type=jnp.float32) + b_in[layer]
        act = gelu_tanh(pre).astype(jnp.bfloat16)
        mixed = (current.astype(jnp.float32) + jnp.dot(act, w_out[layer], preferred_element_type=jnp.float32) + b_out[layer]).astype(jnp.bfloat16)
        current = rotate(mixed, 1)
    result = current
    scale = 1.0 / TOKENS ** 0.5
    grad = cotangent
    gw_in = [None] * LAYERS
    gb_in = [None] * LAYERS
    gw_out = [None] * LAYERS
    gb_out = [None] * LAYERS
    for layer in reversed(range(LAYERS)):
        back = rotate(grad, -1)
        layer_in = inputs[layer]
        pre = jnp.dot(layer_in, w_in[layer], preferred_element_type=jnp.float32) + b_in[layer]
        act = gelu_tanh(pre).astype(jnp.bfloat16)
        grad_act = contract_cols(back, w_out[layer])
        _, pull = jax.vjp(gelu_tanh, pre)
        delta = pull(grad_act)[0].astype(jnp.bfloat16)
        gw_out[layer] = contract_rows(act, back) * scale
        gb_out[layer] = lax.optimization_barrier(jnp.sum(back, axis=0, dtype=jnp.float32)) * scale
        gw_in[layer] = contract_rows(layer_in, delta) * scale
        gb_in[layer] = lax.optimization_barrier(jnp.sum(delta, axis=0, dtype=jnp.float32)) * scale
        grad = (back.astype(jnp.float32) + contract_cols(delta, w_in[layer])).astype(jnp.bfloat16)
    return (result, grad, jnp.stack(gw_in), jnp.stack(gb_in), jnp.stack(gw_out), jnp.stack(gb_out))
```

```python
import functools

import jax
import jax.numpy as jnp
from jax import lax
from jax.experimental import pallas as pl
from jax.experimental.pallas import tpu as pltpu
from jax.sharding import PartitionSpec as P

TRACK_W = 16
LANES = 128
TILE = 512
MESH = pl.DeviceIdType.MESH


def plan(n, rows, width):
    tracks = width // TRACK_W
    total = rows * n
    shifts = [0] + [min(2 ** (t - 1), total // 2) for t in range(1, tracks)]
    near = [t for t in range(1, tracks) if shifts[t] < rows]
    small = [t for t in near if shifts[t] <= LANES]
    groups = []
    for t in range(1, tracks):
        if shifts[t] >= rows:
            hops = (shifts[t] // rows) % n
            if groups and groups[-1][0] == hops:
                groups[-1][2] = t + 1
            else:
                groups.append([hops, t, t + 1])
    return shifts, near, small, groups


def channels(first, last):
    return pl.ds(first * TRACK_W, (last - first) * TRACK_W)


class Rotation:
    def __init__(self, me, n, sign, src, dst, halo, send, recv):
        self.sign, self.src, self.dst, self.halo = sign, src, dst, halo
        width, rows = src.shape
        self.rows = rows
        self.shifts, self.near, self.small, self.groups = plan(n, rows, width)
        self.copies = []

        def add(source, target, hops):
            k = len(self.copies)
            self.copies.append(
                pltpu.make_async_remote_copy(
                    src_ref=source,
                    dst_ref=target,
                    send_sem=send.at[k],
                    recv_sem=recv.at[k],
                    device_id=(lax.rem(me + (sign * hops) % n, n),),
                    device_id_type=MESH,
                )
            )

        for hops, first, last in sorted(self.groups, reverse=True):
            piece = channels(first, last)
            add(src.at[piece, :], dst.at[piece, :], hops)
        wide = [t for t in self.near if t not in self.small]
        for first, last, size in [(t, t + 1, self.shifts[t]) for t in reversed(wide)] + [
            (self.small[0], self.small[-1] + 1, LANES)
        ]:
            start = rows - size if sign > 0 else 0
            piece = channels(first, last)
            add(src.at[piece, pl.ds(start, size)], halo.at[piece, pl.ds(0, size)], 1)

    def start(self):
        for copy in self.copies:
            copy.start()

    def finish(self):
        rows, src, dst, halo = self.rows, self.src, self.dst, self.halo
        for copy in self.copies:
            copy.wait()
        dst[channels(0, 1), :] = src[channels(0, 1), :]
        lane = lax.broadcasted_iota(jnp.int32, (TRACK_W, LANES), 1)
        for t in self.near:
            s, piece = self.shifts[t], channels(t, t + 1)
            if s % LANES == 0:
                if self.sign > 0:
                    dst[piece, pl.ds(s, rows - s)] = src[piece, pl.ds(0, rows - s)]
                    dst[piece, pl.ds(0, s)] = halo[piece, pl.ds(0, s)]
                else:
                    dst[piece, pl.ds(0, rows - s)] = src[piece, pl.ds(s, rows - s)]
                    dst[piece, pl.ds(rows - s, s)] = halo[piece, pl.ds(0, s)]
                continue
            body = src[piece, :].astype(jnp.float32)
            edge = halo[piece, pl.ds(0, LANES)].astype(jnp.float32)
            if self.sign > 0:
                body = pltpu.roll(body, s, 1)
                edge = pltpu.roll(edge, s, 1)
                first = jnp.where(lane < s, edge, body[:, :LANES])
                body = jnp.concatenate([first, body[:, LANES:]], axis=1)
            else:
                body = pltpu.roll(body, rows - s, 1)
                edge = pltpu.roll(edge, LANES - s, 1)
                last = jnp.where(lane >= LANES - s, edge, body[:, rows - LANES :])
                body = jnp.concatenate([body[:, : rows - LANES], last], axis=1)
            dst[piece, :] = body.astype(jnp.bfloat16)


def dot(a, b):
    return jnp.dot(a, b, preferred_element_type=jnp.float32)


def dot_t(a, b):
    return lax.dot_general(a, b, (((1,), (1,)), ((), ())), preferred_element_type=jnp.float32)


def gelu_both(t):
    c = 0.7978845608028654
    sq = t * t
    th = jnp.tanh(c * (t + 0.044715 * (sq * t)))
    half = 0.5 * (1.0 + th)
    slope = half + (0.5 * t) * ((1.0 - th * th) * (c + (3.0 * 0.044715 * c) * sq))
    return half * t, slope


def kernel(
    n, scale, u0, cot, w_in, w_in_t, w_out, w_out_t, b_in, b_out,
    result, grad, reduced,
    back1, m0, u1, m1, r1, g1, back0, halo, act, slope, delta, acc, part, land, own, fin,
    rot_send, rot_recv, rs_send, rs_recv, ag_send, ag_recv,
):
    me = lax.axis_index("seq")
    width, rows = u0.shape
    hidden = w_in_t.shape[1]
    chunk = part.shape[2]
    tile = min(TILE, rows)
    steps = rows // tile

    barrier = pltpu.get_barrier_semaphore()

    def greet(k, carry):
        pl.semaphore_signal(
            barrier, inc=1, device_id=(lax.rem(me + k, n),), device_id_type=MESH
        )
        return carry

    lax.fori_loop(1, n, greet, 0)
    acc[...] = jnp.zeros_like(acc)
    pl.semaphore_wait(barrier, n - 1)

    def rotation(i, sign, src, dst):
        return Rotation(me, n, sign, src, dst, halo.at[i], rot_send.at[i], rot_recv.at[i])

    rot_cot = rotation(0, -1, cot, back1)
    rot_m0 = rotation(1, 1, m0, u1)
    rot_m1 = rotation(2, 1, m1, r1)
    rot_g1 = rotation(3, -1, g1, back0)

    def tiles(body):
        def step(i, carry):
            body(pl.ds(pl.multiple_of(i * tile, tile), tile))
            return carry

        lax.fori_loop(0, steps, step, 0)

    def forward(l, u, out):
        def body(cols):
            x = u[:, cols]
            pre = dot(w_in_t[l], x) + b_in[l]
            a, d = gelu_both(pre)
            a = a.astype(jnp.bfloat16)
            act[l, :, cols] = a
            slope[l, :, cols] = d
            out[:, cols] = (x.astype(jnp.float32) + dot(w_out_t[l], a) + b_out[l]).astype(
                jnp.bfloat16
            )

        tiles(body)

    def backward(l, back, out):
        def body(cols):
            b = back[:, cols]
            d = (dot(w_out[l], b) * slope[l, :, cols]).astype(jnp.bfloat16)
            delta[:, cols] = d
            out[:, cols] = (b.astype(jnp.float32) + dot(w_in[l], d)).astype(jnp.bfloat16)

        tiles(body)

    def weight_grads(l, u, back):
        def body(cols):
            b, d = back[:, cols], delta[:, cols]
            acc[l, pl.ds(0, hidden), pl.ds(0, width)] += dot_t(act[l, :, cols], b)
            acc[l, pl.ds(hidden, hidden), pl.ds(0, width)] += dot_t(d, u[:, cols])
            acc[l, pl.ds(0, width), pl.ds(width, 1)] += jnp.sum(
                b.astype(jnp.float32), axis=1, keepdims=True
            )
            acc[l, pl.ds(hidden, hidden), pl.ds(width, 1)] += jnp.sum(
                d.astype(jnp.float32), axis=1, keepdims=True
            )

        tiles(body)

        def narrow(i, carry):
            part[l, i] = acc[l, pl.ds(pl.multiple_of(i * chunk, 8), chunk), :].astype(jnp.bfloat16)
            return carry

        lax.fori_loop(0, n, narrow, 0)

    def scatter(l, k):
        to = lax.rem(me + k, n)
        return pltpu.make_async_remote_copy(
            src_ref=part.at[l, to],
            dst_ref=land.at[l, k],
            send_sem=rs_send.at[l, k],
            recv_sem=rs_recv.at[l, k],
            device_id=(to,),
            device_id_type=MESH,
        )

    def gather(l, k):
        to = lax.rem(me + k, n)
        return pltpu.make_async_remote_copy(
            src_ref=own.at[l],
            dst_ref=fin.at[l, me],
            send_sem=ag_send.at[l, k],
            recv_sem=ag_recv.at[l, k],
            device_id=(to,),
            device_id_type=MESH,
        )

    def gathered(l, k):
        return pltpu.make_async_remote_copy(
            src_ref=own.at[l],
            dst_ref=fin.at[l, lax.rem(me + n - k, n)],
            send_sem=ag_send.at[l, k],
            recv_sem=ag_recv.at[l, k],
            device_id=(lax.rem(me + k, n),),
            device_id_type=MESH,
        )

    def each(body):
        def step(k, carry):
            body(k)
            return carry

        lax.fori_loop(1, n, step, 0)

    def scatter_start(l):
        each(lambda k: scatter(l, k).start())

    def reduce_and_gather(l):
        each(lambda k: scatter(l, k).wait())

        def add(k, total):
            return total + land[l, k].astype(jnp.float32)

        mine = acc[l, pl.ds(pl.multiple_of(me * chunk, 8), chunk), :]
        total = (lax.fori_loop(1, n, add, mine) * scale).astype(jnp.bfloat16)
        own[l] = total
        fin[l, me] = total
        each(lambda k: gather(l, k).start())

    def gather_finish(l):
        each(lambda k: gathered(l, k).wait())

    rot_cot.start()
    forward(0, u0, m0)
    rot_m0.start()
    rot_cot.finish()
    rot_m0.finish()
    forward(1, u1, m1)
    backward(1, back1, g1)
    rot_g1.start()
    rot_m1.start()
    weight_grads(1, u1, back1)
    rot_g1.finish()
    scatter_start(1)
    backward(0, back0, grad)
    weight_grads(0, u0, back0)
    scatter_start(0)
    rot_m1.finish()
    result[...] = r1[...]
    reduce_and_gather(1)
    reduce_and_gather(0)
    gather_finish(1)
    gather_finish(0)
    reduced[...] = fin[...]


def local(n, tokens, w_in, b_in, w_out, b_out, cotangent):
    rows, width = tokens.shape
    layers, _, hidden = w_in.shape
    scale = 1.0 / (rows * n) ** 0.5
    chunk = -(-2 * hidden // (8 * n)) * 8
    cols = -(-(width + 1) // LANES) * LANES
    shifts, near, small, groups = plan(n, rows, width)
    copies = len(groups) + len(near) - len(small) + 1
    bf16, f32 = jnp.bfloat16, jnp.float32
    vmem = pl.BlockSpec(memory_space=pltpu.VMEM)
    block = pltpu.VMEM((width, rows), bf16)
    result, grad, reduced = pl.pallas_call(
        functools.partial(kernel, n, scale),
        out_shape=[
            jax.ShapeDtypeStruct((width, rows), bf16),
            jax.ShapeDtypeStruct((width, rows), bf16),
            jax.ShapeDtypeStruct((layers, n, chunk, cols), bf16),
        ],
        in_specs=[vmem] * 8,
        out_specs=[vmem] * 3,
        scratch_shapes=[block] * 7
        + [
            pltpu.VMEM((4, (near[-1] + 1) * TRACK_W, rows // 2), bf16),
            pltpu.VMEM((layers, hidden, rows), bf16),
            pltpu.VMEM((layers, hidden, rows), f32),
            pltpu.VMEM((hidden, rows), bf16),
            pltpu.VMEM((layers, n * chunk, cols), f32),
            pltpu.VMEM((layers, n, chunk, cols), bf16),
            pltpu.VMEM((layers, n, chunk, cols), bf16),
            pltpu.VMEM((layers, chunk, cols), bf16),
            pltpu.VMEM((layers, n, chunk, cols), bf16),
            pltpu.SemaphoreType.DMA((4, copies)),
            pltpu.SemaphoreType.DMA((4, copies)),
        ]
        + [pltpu.SemaphoreType.DMA((layers, n))] * 4,
        compiler_params=pltpu.CompilerParams(
            collective_id=0, has_side_effects=True, vmem_limit_bytes=64 * 1024 * 1024 - 65536
        ),
    )(
        tokens.T,
        cotangent.T,
        w_in,
        w_in.transpose(0, 2, 1),
        w_out,
        w_out.transpose(0, 2, 1),
        b_in[:, :, None],
        b_out[:, :, None],
    )
    sums = reduced.reshape(layers, n * chunk, cols).astype(f32)
    return (
        result.T,
        grad.T,
        sums[:, hidden : 2 * hidden, :width].transpose(0, 2, 1),
        sums[:, hidden : 2 * hidden, width],
        sums[:, :hidden, :width],
        sums[:, :width, width],
    )


def solution(mesh):
    return jax.shard_map(
        functools.partial(local, mesh.shape["seq"]),
        mesh=mesh,
        in_specs=(P("seq", None), P(), P(), P(), P(), P("seq", None)),
        out_specs=(P("seq", None), P("seq", None), P(), P(), P(), P()),
        check_vma=False,
    )
```

```python
import functools

import jax
import jax.numpy as jnp
from jax import lax
from jax.experimental import pallas as pl
from jax.experimental.pallas import tpu as pltpu
from jax.sharding import PartitionSpec as P

TRACK_W = 16
LANES = 128
TILE = 512
MESH = pl.DeviceIdType.MESH


def plan(n, rows, width):
    tracks = width // TRACK_W
    total = rows * n
    shifts = [0] + [min(2 ** (t - 1), total // 2) for t in range(1, tracks)]
    near = [t for t in range(1, tracks) if shifts[t] < rows]
    small = [t for t in near if shifts[t] <= LANES]
    groups = []
    for t in range(1, tracks):
        if shifts[t] >= rows:
            hops = (shifts[t] // rows) % n
            if groups and groups[-1][0] == hops:
                groups[-1][2] = t + 1
            else:
                groups.append([hops, t, t + 1])
    return shifts, near, small, groups


def channels(first, last):
    return pl.ds(first * TRACK_W, (last - first) * TRACK_W)


class Rotation:
    def __init__(self, me, n, sign, src, dst, halo, send, recv):
        self.sign, self.src, self.dst, self.halo = sign, src, dst, halo
        width, rows = src.shape
        self.rows = rows
        self.shifts, self.near, self.small, self.groups = plan(n, rows, width)
        self.copies = []

        def add(source, target, hops):
            k = len(self.copies)
            self.copies.append(
                pltpu.make_async_remote_copy(
                    src_ref=source,
                    dst_ref=target,
                    send_sem=send.at[k],
                    recv_sem=recv.at[k],
                    device_id=(lax.rem(me + (sign * hops) % n, n),),
                    device_id_type=MESH,
                )
            )

        for hops, first, last in sorted(self.groups, reverse=True):
            piece = channels(first, last)
            add(src.at[piece, :], dst.at[piece, :], hops)
        wide = [t for t in self.near if t not in self.small]
        for first, last, size in [(t, t + 1, self.shifts[t]) for t in reversed(wide)] + [
            (self.small[0], self.small[-1] + 1, LANES)
        ]:
            start = rows - size if sign > 0 else 0
            piece = channels(first, last)
            add(src.at[piece, pl.ds(start, size)], halo.at[piece, pl.ds(0, size)], 1)

    def start(self):
        for copy in self.copies:
            copy.start()

    def finish(self):
        rows, src, dst, halo = self.rows, self.src, self.dst, self.halo
        for copy in self.copies:
            copy.wait()
        dst[channels(0, 1), :] = src[channels(0, 1), :]
        lane = lax.broadcasted_iota(jnp.int32, (TRACK_W, LANES), 1)
        for t in self.near:
            s, piece = self.shifts[t], channels(t, t + 1)
            if s % LANES == 0:
                if self.sign > 0:
                    dst[piece, pl.ds(s, rows - s)] = src[piece, pl.ds(0, rows - s)]
                    dst[piece, pl.ds(0, s)] = halo[piece, pl.ds(0, s)]
                else:
                    dst[piece, pl.ds(0, rows - s)] = src[piece, pl.ds(s, rows - s)]
                    dst[piece, pl.ds(rows - s, s)] = halo[piece, pl.ds(0, s)]
                continue
            body = src[piece, :].astype(jnp.float32)
            edge = halo[piece, pl.ds(0, LANES)].astype(jnp.float32)
            if self.sign > 0:
                body = pltpu.roll(body, s, 1)
                edge = pltpu.roll(edge, s, 1)
                first = jnp.where(lane < s, edge, body[:, :LANES])
                body = jnp.concatenate([first, body[:, LANES:]], axis=1)
            else:
                body = pltpu.roll(body, rows - s, 1)
                edge = pltpu.roll(edge, LANES - s, 1)
                last = jnp.where(lane >= LANES - s, edge, body[:, rows - LANES :])
                body = jnp.concatenate([body[:, : rows - LANES], last], axis=1)
            dst[piece, :] = body.astype(jnp.bfloat16)


def dot(a, b):
    return jnp.dot(a, b, preferred_element_type=jnp.float32)


def dot_t(a, b):
    return lax.dot_general(a, b, (((1,), (1,)), ((), ())), preferred_element_type=jnp.float32)


def gelu_both(t):
    c = 0.7978845608028654
    sq = t * t
    th = jnp.tanh(c * (t + 0.044715 * (sq * t)))
    half = 0.5 * (1.0 + th)
    slope = half + (0.5 * t) * ((1.0 - th * th) * (c + (3.0 * 0.044715 * c) * sq))
    return half * t, slope


def kernel(
    n, scale, u0, cot, w_in, w_out_t, b_in_row, b_out_row,
    result, grad, reduced,
    back1, m0, u1, m1, r1, g1, back0, w_in_t, w_out, b_in, b_out,
    halo, act, slope, delta, acc, part, land, own, fin,
    rot_send, rot_recv, rs_send, rs_recv, ag_send, ag_recv,
):
    me = lax.axis_index("seq")
    width, rows = u0.shape
    layers, hidden, _ = w_in_t.shape
    owners, chunk = part.shape[1:3]
    tile = min(TILE, rows)
    steps = rows // tile

    barrier = pltpu.get_barrier_semaphore()

    def greet(k, carry):
        pl.semaphore_signal(
            barrier, inc=1, device_id=(lax.rem(me + k, n),), device_id_type=MESH
        )
        return carry

    lax.fori_loop(1, n, greet, 0)
    acc[...] = jnp.zeros_like(acc)
    for l in range(layers):
        w_in_t[l] = w_in[l].T
        w_out[l] = w_out_t[l].T
        for row, column in ((b_in_row, b_in), (b_out_row, b_out)):
            spread = jnp.broadcast_to(row[l : l + 1, :], (LANES, row.shape[1]))
            column[l] = spread.T[:, :1]
    pl.semaphore_wait(barrier, n - 1)

    def rotation(i, sign, src, dst):
        return Rotation(me, n, sign, src, dst, halo.at[i], rot_send.at[i], rot_recv.at[i])

    rot_cot = rotation(0, -1, cot, back1)
    rot_m0 = rotation(1, 1, m0, u1)
    rot_m1 = rotation(2, 1, m1, r1)
    rot_g1 = rotation(3, -1, g1, back0)

    def tiles(body):
        def step(i, carry):
            body(pl.ds(pl.multiple_of(i * tile, tile), tile))
            return carry

        lax.fori_loop(0, steps, step, 0)

    def forward(l, u, out):
        def body(cols):
            x = u[:, cols]
            pre = dot(w_in_t[l], x) + b_in[l]
            a, d = gelu_both(pre)
            a = a.astype(jnp.bfloat16)
            act[l, :, cols] = a
            slope[l, :, cols] = d
            out[:, cols] = (x.astype(jnp.float32) + dot(w_out_t[l], a) + b_out[l]).astype(
                jnp.bfloat16
            )

        tiles(body)

    def backward(l, back, out):
        def body(cols):
            b = back[:, cols]
            d = (dot(w_out[l], b) * slope[l, :, cols]).astype(jnp.bfloat16)
            delta[:, cols] = d
            out[:, cols] = (b.astype(jnp.float32) + dot(w_in[l], d)).astype(jnp.bfloat16)

        tiles(body)

    def weight_grads(l, u, back):
        ones = jnp.ones((TRACK_W, tile), jnp.bfloat16)

        def body(cols):
            b, d = back[:, cols], delta[:, cols]
            acc[l, pl.ds(0, width), :] += dot_t(b, act[l, :, cols])
            acc[l, pl.ds(width, width + TRACK_W), :] += dot_t(
                jnp.concatenate([u[:, cols], ones], axis=0), d
            )
            acc[l, pl.ds(2 * width + TRACK_W, 8), pl.ds(0, width)] += dot_t(ones, b)[:8]

        tiles(body)

        def narrow(i, carry):
            part[l, i] = acc[l, pl.ds(pl.multiple_of(i * chunk, 8), chunk), :].astype(jnp.bfloat16)
            return carry

        lax.fori_loop(0, owners, narrow, 0)

    def scatter(l, k):
        to = lax.rem(me + k, n)
        return pltpu.make_async_remote_copy(
            src_ref=part.at[l, to],
            dst_ref=land.at[l, k],
            send_sem=rs_send.at[l, k],
            recv_sem=rs_recv.at[l, k],
            device_id=(to,),
            device_id_type=MESH,
        )

    def incoming(l, k):
        return pltpu.make_async_remote_copy(
            src_ref=own.at[l],
            dst_ref=land.at[l, k],
            send_sem=rs_send.at[l, k],
            recv_sem=rs_recv.at[l, k],
            device_id=(lax.rem(me + k, n),),
            device_id_type=MESH,
        )

    def gather(l, k, slot):
        return pltpu.make_async_remote_copy(
            src_ref=own.at[l],
            dst_ref=fin.at[l, slot],
            send_sem=ag_send.at[l, k],
            recv_sem=ag_recv.at[l, k],
            device_id=(lax.rem(me + k, n),),
            device_id_type=MESH,
        )

    def each(body):
        def step(k, carry):
            body(k)
            return carry

        lax.fori_loop(1, n, step, 0)

    def to_owner(body):
        def guarded(k):
            @pl.when(lax.rem(me + k, n) < owners)
            def _():
                body(k)

        each(guarded)

    def scatter_start(l):
        to_owner(lambda k: scatter(l, k).start())

    def reduce_and_gather(l):
        @pl.when(me < owners)
        def _():
            each(lambda k: incoming(l, k).wait_recv())

            def add(k, total):
                return total + land[l, k].astype(jnp.float32)

            mine = acc[l, pl.ds(pl.multiple_of(me * chunk, 8), chunk), :]
            total = (lax.fori_loop(1, n, add, mine) * scale).astype(jnp.bfloat16)
            own[l] = total
            fin[l, me] = total
            each(lambda k: gather(l, k, me).start())

    def gather_finish(l):
        to_owner(lambda k: scatter(l, k).wait_send())

        @pl.when(me < owners)
        def _():
            each(lambda k: gather(l, k, me).wait_send())

        def arrive(k):
            source = lax.rem(me + n - k, n)

            @pl.when(source < owners)
            def _():
                gather(l, k, source).wait_recv()

        each(arrive)

    rot_cot.start()
    forward(0, u0, m0)
    rot_m0.start()
    rot_cot.finish()
    rot_m0.finish()
    forward(1, u1, m1)
    backward(1, back1, g1)
    rot_g1.start()
    rot_m1.start()
    weight_grads(1, u1, back1)
    rot_g1.finish()
    scatter_start(1)
    backward(0, back0, grad)
    weight_grads(0, u0, back0)
    scatter_start(0)
    rot_m1.finish()
    result[...] = r1[...]
    reduce_and_gather(1)
    reduce_and_gather(0)
    gather_finish(1)
    gather_finish(0)
    reduced[...] = fin[...]


def local(n, tokens, w_in, b_in, w_out, b_out, cotangent):
    rows, width = tokens.shape
    layers, _, hidden = w_in.shape
    scale = 1.0 / (rows * n) ** 0.5
    needed = 2 * width + TRACK_W + 8
    chunk = -(-needed // (8 * n)) * 8
    owners = -(-needed // chunk)
    shifts, near, small, groups = plan(n, rows, width)
    copies = len(groups) + len(near) - len(small) + 1
    bf16, f32 = jnp.bfloat16, jnp.float32
    vmem = pl.BlockSpec(memory_space=pltpu.VMEM)
    block = pltpu.VMEM((width, rows), bf16)
    result, grad, reduced = pl.pallas_call(
        functools.partial(kernel, n, scale),
        out_shape=[
            jax.ShapeDtypeStruct((width, rows), bf16),
            jax.ShapeDtypeStruct((width, rows), bf16),
            jax.ShapeDtypeStruct((layers, owners, chunk, hidden), bf16),
        ],
        in_specs=[vmem] * 6,
        out_specs=[vmem] * 3,
        scratch_shapes=[block] * 7
        + [
            pltpu.VMEM((layers, hidden, width), bf16),
            pltpu.VMEM((layers, hidden, width), bf16),
            pltpu.VMEM((layers, hidden, 1), f32),
            pltpu.VMEM((layers, width, 1), f32),
            pltpu.VMEM((4, (near[-1] + 1) * TRACK_W, rows // 2), bf16),
            pltpu.VMEM((layers, hidden, rows), bf16),
            pltpu.VMEM((layers, hidden, rows), f32),
            pltpu.VMEM((hidden, rows), bf16),
            pltpu.VMEM((layers, owners * chunk, hidden), f32),
            pltpu.VMEM((layers, owners, chunk, hidden), bf16),
            pltpu.VMEM((layers, n, chunk, hidden), bf16),
            pltpu.VMEM((layers, chunk, hidden), bf16),
            pltpu.VMEM((layers, owners, chunk, hidden), bf16),
            pltpu.SemaphoreType.DMA((4, copies)),
            pltpu.SemaphoreType.DMA((4, copies)),
        ]
        + [pltpu.SemaphoreType.DMA((layers, n))] * 4,
        compiler_params=pltpu.CompilerParams(
            collective_id=0, has_side_effects=True, vmem_limit_bytes=64 * 1024 * 1024 - 65536
        ),
    )(
        tokens.T,
        cotangent.T,
        w_in,
        w_out.transpose(0, 2, 1),
        b_in,
        b_out,
    )
    sums = reduced.reshape(layers, owners * chunk, hidden).astype(f32)
    return (
        result.T,
        grad.T,
        sums[:, width : 2 * width],
        sums[:, 2 * width],
        sums[:, :width].transpose(0, 2, 1),
        sums[:, 2 * width + TRACK_W, :width],
    )


def solution(mesh):
    return jax.shard_map(
        functools.partial(local, mesh.shape["seq"]),
        mesh=mesh,
        in_specs=(P("seq", None), P(), P(), P(), P(), P("seq", None)),
        out_specs=(P("seq", None), P("seq", None), P(), P(), P(), P()),
        check_vma=False,
    )
```

```python
import functools

import jax
import jax.numpy as jnp
from jax import lax
from jax.experimental import pallas as pl
from jax.experimental.pallas import tpu as pltpu
from jax.sharding import PartitionSpec as P

TRACK_W = 16
LANES = 128
TILE = 512
MESH = pl.DeviceIdType.MESH


def plan(n, rows, width):
    tracks = width // TRACK_W
    total = rows * n
    shifts = [0] + [min(2 ** (t - 1), total // 2) for t in range(1, tracks)]
    near = [t for t in range(1, tracks) if shifts[t] < rows]
    small = [t for t in near if shifts[t] <= LANES]
    groups = []
    for t in range(1, tracks):
        if shifts[t] >= rows:
            hops = (shifts[t] // rows) % n
            if groups and groups[-1][0] == hops:
                groups[-1][2] = t + 1
            else:
                groups.append([hops, t, t + 1])
    return shifts, near, small, groups


def channels(first, last):
    return pl.ds(first * TRACK_W, (last - first) * TRACK_W)


def radices(n):
    factors = []
    for factor in [2] + [4] * 16 + [2] * 2:
        if n % factor == 0 and n > 1:
            factors.append(factor)
            n //= factor
    if n > 1:
        factors.append(n)
    return factors


class Rotation:
    def __init__(self, me, n, sign, src, dst, halo, send, recv):
        self.sign, self.src, self.dst, self.halo = sign, src, dst, halo
        width, rows = src.shape
        self.rows = rows
        self.shifts, self.near, self.small, self.groups = plan(n, rows, width)
        self.copies = []

        def add(source, target, hops):
            k = len(self.copies)
            self.copies.append(
                pltpu.make_async_remote_copy(
                    src_ref=source,
                    dst_ref=target,
                    send_sem=send.at[k],
                    recv_sem=recv.at[k],
                    device_id=(lax.rem(me + (sign * hops) % n, n),),
                    device_id_type=MESH,
                )
            )

        for hops, first, last in sorted(self.groups, reverse=True):
            piece = channels(first, last)
            add(src.at[piece, :], dst.at[piece, :], hops)
        wide = [t for t in self.near if t not in self.small]
        for first, last, size in [(t, t + 1, self.shifts[t]) for t in reversed(wide)] + [
            (self.small[0], self.small[-1] + 1, LANES)
        ]:
            start = rows - size if sign > 0 else 0
            piece = channels(first, last)
            add(src.at[piece, pl.ds(start, size)], halo.at[piece, pl.ds(0, size)], 1)

    def start(self):
        for copy in self.copies:
            copy.start()

    def finish(self):
        rows, src, dst, halo = self.rows, self.src, self.dst, self.halo
        for copy in self.copies:
            copy.wait()
        dst[channels(0, 1), :] = src[channels(0, 1), :]
        lane = lax.broadcasted_iota(jnp.int32, (TRACK_W, LANES), 1)
        for t in self.near:
            s, piece = self.shifts[t], channels(t, t + 1)
            if s % LANES == 0:
                if self.sign > 0:
                    dst[piece, pl.ds(s, rows - s)] = src[piece, pl.ds(0, rows - s)]
                    dst[piece, pl.ds(0, s)] = halo[piece, pl.ds(0, s)]
                else:
                    dst[piece, pl.ds(0, rows - s)] = src[piece, pl.ds(s, rows - s)]
                    dst[piece, pl.ds(rows - s, s)] = halo[piece, pl.ds(0, s)]
                continue
            body = src[piece, :].astype(jnp.float32)
            edge = halo[piece, pl.ds(0, LANES)].astype(jnp.float32)
            if self.sign > 0:
                body = pltpu.roll(body, s, 1)
                edge = pltpu.roll(edge, s, 1)
                first = jnp.where(lane < s, edge, body[:, :LANES])
                body = jnp.concatenate([first, body[:, LANES:]], axis=1)
            else:
                body = pltpu.roll(body, rows - s, 1)
                edge = pltpu.roll(edge, LANES - s, 1)
                last = jnp.where(lane >= LANES - s, edge, body[:, rows - LANES :])
                body = jnp.concatenate([body[:, : rows - LANES], last], axis=1)
            dst[piece, :] = body.astype(jnp.bfloat16)


def dot(a, b):
    return jnp.dot(a, b, preferred_element_type=jnp.float32)


def dot_t(a, b):
    return lax.dot_general(a, b, (((1,), (1,)), ((), ())), preferred_element_type=jnp.float32)


def gelu_both(t):
    c = 0.7978845608028654
    sq = t * t
    th = jnp.tanh(c * (t + 0.044715 * (sq * t)))
    half = 0.5 * (1.0 + th)
    slope = half + (0.5 * t) * ((1.0 - th * th) * (c + (3.0 * 0.044715 * c) * sq))
    return half * t, slope


def kernel(
    n, scale, u0, cot, w_in, w_out_t, b_in_row, b_out_row,
    result, grad, reduced,
    back1, u1, r1, back0, w_in_t, w_out, b_in, b_out,
    halo, act, slope, delta, acc, part, land, own, fin,
    rot_send, rot_recv, rs_send, rs_recv, ag_send, ag_recv,
):
    me = lax.axis_index("seq")
    m0, m1, g1 = result, result, grad
    width, rows = u0.shape
    layers, hidden, _ = w_in_t.shape
    chunk = part.shape[2]
    tile = min(TILE, rows)
    steps = rows // tile

    barrier = pltpu.get_barrier_semaphore()

    def greet(k, carry):
        pl.semaphore_signal(
            barrier, inc=1, device_id=(lax.rem(me + k, n),), device_id_type=MESH
        )
        return carry

    lax.fori_loop(1, n, greet, 0)
    acc[...] = jnp.zeros_like(acc)
    for l in range(layers):
        w_in_t[l] = w_in[l].T
        w_out[l] = w_out_t[l].T
        for row, column in ((b_in_row, b_in), (b_out_row, b_out)):
            spread = jnp.broadcast_to(row[l : l + 1, :], (LANES, row.shape[1]))
            column[l] = spread.T[:, :1]
    pl.semaphore_wait(barrier, n - 1)

    def rotation(i, sign, src, dst):
        return Rotation(me, n, sign, src, dst, halo.at[i], rot_send.at[i], rot_recv.at[i])

    rot_cot = rotation(0, -1, cot, back1)
    rot_m0 = rotation(1, 1, m0, u1)
    rot_m1 = rotation(2, 1, m1, r1)
    rot_g1 = rotation(3, -1, g1, back0)

    def tiles(body):
        def step(i, carry):
            body(pl.ds(pl.multiple_of(i * tile, tile), tile))
            return carry

        lax.fori_loop(0, steps, step, 0)

    def forward(l, u, out):
        def body(cols):
            x = u[:, cols]
            pre = dot(w_in_t[l], x) + b_in[l]
            a, d = gelu_both(pre)
            a = a.astype(jnp.bfloat16)
            act[l, :, cols] = a
            slope[l, :, cols] = d
            out[:, cols] = (x.astype(jnp.float32) + dot(w_out_t[l], a) + b_out[l]).astype(
                jnp.bfloat16
            )

        tiles(body)

    def backward(l, back, out):
        def body(cols):
            b = back[:, cols]
            d = (dot(w_out[l], b) * slope[l, :, cols]).astype(jnp.bfloat16)
            delta[:, cols] = d
            out[:, cols] = (b.astype(jnp.float32) + dot(w_in[l], d)).astype(jnp.bfloat16)

        tiles(body)

    def weight_grads(l, u, back):
        ones = jnp.ones((TRACK_W, tile), jnp.bfloat16)

        def body(cols):
            b, d = back[:, cols], delta[:, cols]
            acc[l, pl.ds(0, width), :] += dot_t(b, act[l, :, cols])
            acc[l, pl.ds(width, width + TRACK_W), :] += dot_t(
                jnp.concatenate([u[:, cols], ones], axis=0), d
            )
            acc[l, pl.ds(2 * width + TRACK_W, 8), pl.ds(0, width)] += dot_t(ones, b)[:8]

        tiles(body)

    stages, stride, length, first, offset = [], 1, n, 0, 0
    for radix in radices(n):
        digit = lax.rem(me // stride, radix)
        share = length // radix
        mine = first + digit * share
        stages.append((radix, stride, digit, share, first, mine, offset))
        first, length, stride, offset = mine, share, stride * radix, offset + (radix - 1) * share
    last = len(stages) - 1

    def rows_of(i):
        return pl.ds(pl.multiple_of(i * chunk, 8), chunk)

    def exchange(s, j, src, dst, sends, recvs):
        radix, stride, digit = stages[s][:3]
        return pltpu.make_async_remote_copy(
            src_ref=src,
            dst_ref=dst,
            send_sem=sends.at[s, j],
            recv_sem=recvs.at[s, j],
            device_id=(me + (lax.rem(digit + j, radix) - digit) * stride,),
            device_id_type=MESH,
        )

    def scatter(l, s):
        radix, _, digit, share, first, _, offset = stages[s]
        return [
            exchange(
                s, j,
                part.at[l, pl.ds(first + lax.rem(digit + j, radix) * share, share)],
                land.at[l, pl.ds(offset + (j - 1) * share, share)],
                rs_send.at[l], rs_recv.at[l],
            )
            for j in range(1, radix)
        ]

    def gather(l, s, arriving):
        radix, _, digit, share, first, mine, _ = stages[s]
        return [
            exchange(
                s, j,
                fin.at[l, pl.ds(mine, share)],
                fin.at[
                    l,
                    pl.ds(first + lax.rem(digit + radix - j, radix) * share, share)
                    if arriving
                    else pl.ds(mine, share),
                ],
                ag_send.at[l], ag_recv.at[l],
            )
            for j in range(1, radix)
        ]

    def scatter_start(l):
        def narrow(i, carry):
            part[l, i] = acc[l, rows_of(i), :].astype(jnp.bfloat16)
            return carry

        lax.fori_loop(0, n, narrow, 0)
        for copy in scatter(l, 0):
            copy.start()

    def scatter_step(l, s):
        radix, _, _, share, _, mine, offset = stages[s]
        for copy in scatter(l, s):
            copy.wait()

        def add(i, carry):
            total = acc[l, rows_of(mine + i), :]
            for j in range(radix - 1):
                total = total + land[l, offset + j * share + i].astype(jnp.float32)
            if s < last:
                acc[l, rows_of(mine + i), :] = total
                part[l, mine + i] = total.astype(jnp.bfloat16)
            else:
                fin[l, mine + i] = (total * scale).astype(jnp.bfloat16)
            return carry

        lax.fori_loop(0, share, add, 0)
        for copy in scatter(l, s + 1) if s < last else gather(l, last, False):
            copy.start()

    def gather_step(l, s):
        for copy in gather(l, s, True):
            copy.wait()
        if s > 0:
            for copy in gather(l, s - 1, False):
                copy.start()

    rot_cot.start()
    forward(0, u0, m0)
    rot_m0.start()
    rot_cot.finish()
    rot_m0.finish()
    forward(1, u1, m1)
    backward(1, back1, g1)
    rot_g1.start()
    weight_grads(1, u1, back1)
    scatter_start(1)
    rot_g1.finish()
    rot_m1.start()
    backward(0, back0, grad)
    todo = [functools.partial(scatter_step, s=s) for s in range(last + 1)]
    todo += [functools.partial(gather_step, s=s) for s in reversed(range(last + 1))]
    todo[0](1)
    weight_grads(0, u0, back0)
    scatter_start(0)
    todo[1](1)
    rot_m1.finish()
    result[...] = r1[...]
    for step in range(len(todo)):
        todo[step](0)
        if step + 2 < len(todo):
            todo[step + 2](1)
    reduced[...] = fin[...]


def local(n, tokens, w_in, b_in, w_out, b_out, cotangent):
    rows, width = tokens.shape
    layers, _, hidden = w_in.shape
    scale = 1.0 / (rows * n) ** 0.5
    needed = 2 * width + TRACK_W + 8
    chunk = -(-needed // (8 * n)) * 8
    shifts, near, small, groups = plan(n, rows, width)
    factors = radices(n)
    copies = len(groups) + len(near) - len(small) + 1
    bf16, f32 = jnp.bfloat16, jnp.float32
    vmem = pl.BlockSpec(memory_space=pltpu.VMEM)
    block = pltpu.VMEM((width, rows), bf16)
    result, grad, reduced = pl.pallas_call(
        functools.partial(kernel, n, scale),
        out_shape=[
            jax.ShapeDtypeStruct((width, rows), bf16),
            jax.ShapeDtypeStruct((width, rows), bf16),
            jax.ShapeDtypeStruct((layers, n, chunk, hidden), bf16),
        ],
        in_specs=[vmem] * 6,
        out_specs=[vmem] * 3,
        scratch_shapes=[block] * 4
        + [
            pltpu.VMEM((layers, hidden, width), bf16),
            pltpu.VMEM((layers, hidden, width), bf16),
            pltpu.VMEM((layers, hidden, 1), f32),
            pltpu.VMEM((layers, width, 1), f32),
            pltpu.VMEM((4, (near[-1] + 1) * TRACK_W, rows // 2), bf16),
            pltpu.VMEM((layers, hidden, rows), bf16),
            pltpu.VMEM((layers, hidden, rows), f32),
            pltpu.VMEM((hidden, rows), bf16),
            pltpu.VMEM((layers, n * chunk, hidden), f32),
            pltpu.VMEM((layers, n, chunk, hidden), bf16),
            pltpu.VMEM((layers, n, chunk, hidden), bf16),
            pltpu.VMEM((layers, chunk, hidden), bf16),
            pltpu.VMEM((layers, n, chunk, hidden), bf16),
            pltpu.SemaphoreType.DMA((4, copies)),
            pltpu.SemaphoreType.DMA((4, copies)),
        ]
        + [pltpu.SemaphoreType.DMA((layers, len(factors), max(factors)))] * 4,
        compiler_params=pltpu.CompilerParams(
            collective_id=0, has_side_effects=True, vmem_limit_bytes=64 * 1024 * 1024 - 65536
        ),
    )(
        tokens.T,
        cotangent.T,
        w_in,
        w_out.transpose(0, 2, 1),
        b_in,
        b_out,
    )
    sums = reduced.reshape(layers, n * chunk, hidden).astype(f32)
    return (
        result.T,
        grad.T,
        sums[:, width : 2 * width],
        sums[:, 2 * width],
        sums[:, :width].transpose(0, 2, 1),
        sums[:, 2 * width + TRACK_W, :width],
    )


def solution(mesh):
    return jax.shard_map(
        functools.partial(local, mesh.shape["seq"]),
        mesh=mesh,
        in_specs=(P("seq", None), P(), P(), P(), P(), P("seq", None)),
        out_specs=(P("seq", None), P("seq", None), P(), P(), P(), P()),
        check_vma=False,
    )
```

```python
import functools

import jax
import jax.numpy as jnp
from jax import lax
from jax.experimental import pallas as pl
from jax.experimental.pallas import tpu as pltpu
from jax.sharding import PartitionSpec as P

TRACK_W = 16
LANES = 128
TILE = 512
MESH = pl.DeviceIdType.MESH


def plan(n, rows, width):
    tracks = width // TRACK_W
    total = rows * n
    shifts = [0] + [min(2 ** (t - 1), total // 2) for t in range(1, tracks)]
    near = [t for t in range(1, tracks) if shifts[t] < rows]
    small = [t for t in near if shifts[t] <= LANES]
    groups = []
    for t in range(1, tracks):
        if shifts[t] >= rows:
            hops = (shifts[t] // rows) % n
            if groups and groups[-1][0] == hops:
                groups[-1][2] = t + 1
            else:
                groups.append([hops, t, t + 1])
    return shifts, near, small, groups


def channels(first, last):
    return pl.ds(first * TRACK_W, (last - first) * TRACK_W)


def radices(n):
    factors = []
    for factor in [2] + [4] * 16 + [2] * 2:
        if n % factor == 0 and n > 1:
            factors.append(factor)
            n //= factor
    if n > 1:
        factors.append(n)
    return factors


def halfway(n, groups):
    for hops, first, last in groups:
        if 2 * hops == n and n % 4 == 0 and last - first > 1:
            return list(range(first, last))
    return []


class Rotation:
    def __init__(self, me, n, sign, src, dst, halo, relay, send, recv):
        self.sign, self.src, self.dst, self.halo = sign, src, dst, halo
        width, rows = src.shape
        self.rows = rows
        self.shifts, self.near, self.small, self.groups = plan(n, rows, width)
        self.copies, self.onward = [], []
        split = halfway(n, self.groups)

        def add(source, target, hops, direction=sign, into=self.copies):
            k = len(self.copies) + len(self.onward)
            into.append(
                pltpu.make_async_remote_copy(
                    src_ref=source,
                    dst_ref=target,
                    send_sem=send.at[k],
                    recv_sem=recv.at[k],
                    device_id=(lax.rem(me + (direction * hops) % n, n),),
                    device_id_type=MESH,
                )
            )

        for i, t in enumerate(split):
            piece, stop = channels(t, t + 1), relay.at[channels(i, i + 1), :]
            way = 1 if i % 2 == 0 else -1
            add(src.at[piece, :], stop, n // 4, way)
            add(stop, dst.at[piece, :], n // 4, way, self.onward)
        for hops, first, last in sorted(self.groups, reverse=True):
            if first in split:
                continue
            piece = channels(first, last)
            add(src.at[piece, :], dst.at[piece, :], hops)
        wide = [t for t in self.near if t not in self.small]
        for first, last, size in [(t, t + 1, self.shifts[t]) for t in reversed(wide)] + [
            (self.small[0], self.small[-1] + 1, LANES)
        ]:
            start = rows - size if sign > 0 else 0
            piece = channels(first, last)
            add(src.at[piece, pl.ds(start, size)], halo.at[piece, pl.ds(0, size)], 1)

    def start(self):
        for copy in self.copies:
            copy.start()

    def pass_on(self):
        for first, second in zip(self.copies, self.onward):
            first.wait_recv()
            second.start()

    def finish(self):
        rows, src, dst, halo = self.rows, self.src, self.dst, self.halo
        for i, copy in enumerate(self.copies):
            if i < len(self.onward):
                copy.wait_send()
            else:
                copy.wait()
        for copy in self.onward:
            copy.wait()
        dst[channels(0, 1), :] = src[channels(0, 1), :]
        lane = lax.broadcasted_iota(jnp.int32, (TRACK_W, LANES), 1)
        for t in self.near:
            s, piece = self.shifts[t], channels(t, t + 1)
            if s % LANES == 0:
                if self.sign > 0:
                    dst[piece, pl.ds(s, rows - s)] = src[piece, pl.ds(0, rows - s)]
                    dst[piece, pl.ds(0, s)] = halo[piece, pl.ds(0, s)]
                else:
                    dst[piece, pl.ds(0, rows - s)] = src[piece, pl.ds(s, rows - s)]
                    dst[piece, pl.ds(rows - s, s)] = halo[piece, pl.ds(0, s)]
                continue
            body = src[piece, :].astype(jnp.float32)
            edge = halo[piece, pl.ds(0, LANES)].astype(jnp.float32)
            if self.sign > 0:
                body = pltpu.roll(body, s, 1)
                edge = pltpu.roll(edge, s, 1)
                first = jnp.where(lane < s, edge, body[:, :LANES])
                body = jnp.concatenate([first, body[:, LANES:]], axis=1)
            else:
                body = pltpu.roll(body, rows - s, 1)
                edge = pltpu.roll(edge, LANES - s, 1)
                last = jnp.where(lane >= LANES - s, edge, body[:, rows - LANES :])
                body = jnp.concatenate([body[:, : rows - LANES], last], axis=1)
            dst[piece, :] = body.astype(jnp.bfloat16)


def dot(a, b):
    return jnp.dot(a, b, preferred_element_type=jnp.float32)


def dot_t(a, b):
    return lax.dot_general(a, b, (((1,), (1,)), ((), ())), preferred_element_type=jnp.float32)


def gelu_both(t):
    c = 0.7978845608028654
    sq = t * t
    th = jnp.tanh(c * (t + 0.044715 * (sq * t)))
    half = 0.5 * (1.0 + th)
    slope = half + (0.5 * t) * ((1.0 - th * th) * (c + (3.0 * 0.044715 * c) * sq))
    return half * t, slope


def kernel(
    n, scale, u0, cot, w_in, w_out_t, b_in_row, b_out_row,
    result, grad, reduced,
    back1, u1, r1, back0, w_in_t, w_out, b_in, b_out,
    halo, relay, act, slope, delta, acc, part, land, own, fin,
    rot_send, rot_recv, rs_send, rs_recv, ag_send, ag_recv,
):
    me = lax.axis_index("seq")
    m0, m1, g1 = result, result, grad
    width, rows = u0.shape
    layers, hidden, _ = w_in_t.shape
    chunk = part.shape[2]
    tile = min(TILE, rows)
    steps = rows // tile

    barrier = pltpu.get_barrier_semaphore()

    def greet(k, carry):
        pl.semaphore_signal(
            barrier, inc=1, device_id=(lax.rem(me + k, n),), device_id_type=MESH
        )
        return carry

    lax.fori_loop(1, n, greet, 0)
    acc[...] = jnp.zeros_like(acc)
    for l in range(layers):
        w_in_t[l] = w_in[l].T
        w_out[l] = w_out_t[l].T
        for row, column in ((b_in_row, b_in), (b_out_row, b_out)):
            spread = jnp.broadcast_to(row[l : l + 1, :], (LANES, row.shape[1]))
            column[l] = spread.T[:, :1]
    pl.semaphore_wait(barrier, n - 1)

    def rotation(i, sign, src, dst):
        return Rotation(me, n, sign, src, dst, halo.at[i], relay.at[i], rot_send.at[i], rot_recv.at[i])

    rot_cot = rotation(0, -1, cot, back1)
    rot_m0 = rotation(1, 1, m0, u1)
    rot_m1 = rotation(2, 1, m1, r1)
    rot_g1 = rotation(3, -1, g1, back0)

    def tiles(body, between=None):
        def step(i, carry):
            body(pl.ds(pl.multiple_of(i * tile, tile), tile))
            return carry

        middle = steps // 2 if between else 0
        if between:
            lax.fori_loop(0, middle, step, 0)
            between()
        lax.fori_loop(middle, steps, step, 0)

    def forward(l, u, out):
        def body(cols):
            x = u[:, cols]
            pre = dot(w_in_t[l], x) + b_in[l]
            a, d = gelu_both(pre)
            a = a.astype(jnp.bfloat16)
            act[l, :, cols] = a
            slope[l, :, cols] = d
            out[:, cols] = (x.astype(jnp.float32) + dot(w_out_t[l], a) + b_out[l]).astype(
                jnp.bfloat16
            )

        tiles(body)

    def backward(l, back, out):
        def body(cols):
            b = back[:, cols]
            d = (dot(w_out[l], b) * slope[l, :, cols]).astype(jnp.bfloat16)
            delta[:, cols] = d
            out[:, cols] = (b.astype(jnp.float32) + dot(w_in[l], d)).astype(jnp.bfloat16)

        tiles(body)

    def weight_grads(l, u, back, between=None):
        ones = jnp.ones((TRACK_W, tile), jnp.bfloat16)

        def body(cols):
            b, d = back[:, cols], delta[:, cols]
            acc[l, pl.ds(0, width), :] += dot_t(b, act[l, :, cols])
            acc[l, pl.ds(width, width + TRACK_W), :] += dot_t(
                jnp.concatenate([u[:, cols], ones], axis=0), d
            )
            acc[l, pl.ds(2 * width + TRACK_W, 8), pl.ds(0, width)] += dot_t(ones, b)[:8]

        tiles(body, between)

    stages, stride, length, first, offset = [], 1, n, 0, 0
    for radix in radices(n):
        digit = lax.rem(me // stride, radix)
        share = length // radix
        mine = first + digit * share
        stages.append((radix, stride, digit, share, first, mine, offset))
        first, length, stride, offset = mine, share, stride * radix, offset + (radix - 1) * share
    last = len(stages) - 1

    def rows_of(i):
        return pl.ds(pl.multiple_of(i * chunk, 8), chunk)

    def exchange(s, j, src, dst, sends, recvs):
        radix, stride, digit = stages[s][:3]
        return pltpu.make_async_remote_copy(
            src_ref=src,
            dst_ref=dst,
            send_sem=sends.at[s, j],
            recv_sem=recvs.at[s, j],
            device_id=(me + (lax.rem(digit + j, radix) - digit) * stride,),
            device_id_type=MESH,
        )

    def scatter(l, s):
        radix, _, digit, share, first, _, offset = stages[s]
        return [
            exchange(
                s, j,
                part.at[l, pl.ds(first + lax.rem(digit + j, radix) * share, share)],
                land.at[l, pl.ds(offset + (j - 1) * share, share)],
                rs_send.at[l], rs_recv.at[l],
            )
            for j in range(1, radix)
        ]

    def gather(l, s, arriving):
        radix, _, digit, share, first, mine, _ = stages[s]
        return [
            exchange(
                s, j,
                fin.at[l, pl.ds(mine, share)],
                fin.at[
                    l,
                    pl.ds(first + lax.rem(digit + radix - j, radix) * share, share)
                    if arriving
                    else pl.ds(mine, share),
                ],
                ag_send.at[l], ag_recv.at[l],
            )
            for j in range(1, radix)
        ]

    def scatter_start(l):
        def narrow(i, carry):
            part[l, i] = acc[l, rows_of(i), :].astype(jnp.bfloat16)
            return carry

        lax.fori_loop(0, n, narrow, 0)
        for copy in scatter(l, 0):
            copy.start()

    def scatter_step(l, s):
        radix, _, _, share, _, mine, offset = stages[s]
        for copy in scatter(l, s):
            copy.wait()

        def add(i, carry):
            total = acc[l, rows_of(mine + i), :]
            for j in range(radix - 1):
                total = total + land[l, offset + j * share + i].astype(jnp.float32)
            if s < last:
                acc[l, rows_of(mine + i), :] = total
                part[l, mine + i] = total.astype(jnp.bfloat16)
            else:
                fin[l, mine + i] = (total * scale).astype(jnp.bfloat16)
            return carry

        lax.fori_loop(0, share, add, 0)
        for copy in scatter(l, s + 1) if s < last else gather(l, last, False):
            copy.start()

    def gather_step(l, s):
        for copy in gather(l, s, True):
            copy.wait()
        if s > 0:
            for copy in gather(l, s - 1, False):
                copy.start()

    rot_cot.start()
    forward(0, u0, m0)
    rot_m0.start()
    rot_cot.pass_on()
    rot_m0.pass_on()
    rot_cot.finish()
    rot_m0.finish()
    forward(1, u1, m1)
    backward(1, back1, g1)
    rot_g1.start()
    weight_grads(1, u1, back1, rot_g1.pass_on)
    scatter_start(1)
    rot_g1.finish()
    rot_m1.start()
    backward(0, back0, grad)
    rot_m1.pass_on()
    todo = [functools.partial(scatter_step, s=s) for s in range(last + 1)]
    todo += [functools.partial(gather_step, s=s) for s in reversed(range(last + 1))]
    todo[0](1)
    weight_grads(0, u0, back0)
    scatter_start(0)
    todo[1](1)
    rot_m1.finish()
    result[...] = r1[...]
    for step in range(len(todo)):
        todo[step](0)
        if step + 2 < len(todo):
            todo[step + 2](1)
    reduced[...] = fin[...]


def local(n, tokens, w_in, b_in, w_out, b_out, cotangent):
    rows, width = tokens.shape
    layers, _, hidden = w_in.shape
    scale = 1.0 / (rows * n) ** 0.5
    needed = 2 * width + TRACK_W + 8
    chunk = -(-needed // (8 * n)) * 8
    shifts, near, small, groups = plan(n, rows, width)
    factors = radices(n)
    copies = len(groups) + len(near) - len(small) + 1 + 2 * len(halfway(n, groups))
    bf16, f32 = jnp.bfloat16, jnp.float32
    vmem = pl.BlockSpec(memory_space=pltpu.VMEM)
    block = pltpu.VMEM((width, rows), bf16)
    result, grad, reduced = pl.pallas_call(
        functools.partial(kernel, n, scale),
        out_shape=[
            jax.ShapeDtypeStruct((width, rows), bf16),
            jax.ShapeDtypeStruct((width, rows), bf16),
            jax.ShapeDtypeStruct((layers, n, chunk, hidden), bf16),
        ],
        in_specs=[vmem] * 6,
        out_specs=[vmem] * 3,
        scratch_shapes=[block] * 4
        + [
            pltpu.VMEM((layers, hidden, width), bf16),
            pltpu.VMEM((layers, hidden, width), bf16),
            pltpu.VMEM((layers, hidden, 1), f32),
            pltpu.VMEM((layers, width, 1), f32),
            pltpu.VMEM((4, (near[-1] + 1) * TRACK_W, rows // 2), bf16),
            pltpu.VMEM((4, max(len(halfway(n, groups)), 1) * TRACK_W, rows), bf16)
            if halfway(n, groups)
            else pltpu.VMEM((4, TRACK_W, LANES), bf16),
            pltpu.VMEM((layers, hidden, rows), bf16),
            pltpu.VMEM((layers, hidden, rows), f32),
            pltpu.VMEM((hidden, rows), bf16),
            pltpu.VMEM((layers, n * chunk, hidden), f32),
            pltpu.VMEM((layers, n, chunk, hidden), bf16),
            pltpu.VMEM((layers, n, chunk, hidden), bf16),
            pltpu.VMEM((layers, chunk, hidden), bf16),
            pltpu.VMEM((layers, n, chunk, hidden), bf16),
            pltpu.SemaphoreType.DMA((4, copies)),
            pltpu.SemaphoreType.DMA((4, copies)),
        ]
        + [pltpu.SemaphoreType.DMA((layers, len(factors), max(factors)))] * 4,
        compiler_params=pltpu.CompilerParams(
            collective_id=0, has_side_effects=True, vmem_limit_bytes=64 * 1024 * 1024 - 65536
        ),
    )(
        tokens.T,
        cotangent.T,
        w_in,
        w_out.transpose(0, 2, 1),
        b_in,
        b_out,
    )
    sums = reduced.reshape(layers, n * chunk, hidden).astype(f32)
    return (
        result.T,
        grad.T,
        sums[:, width : 2 * width],
        sums[:, 2 * width],
        sums[:, :width].transpose(0, 2, 1),
        sums[:, 2 * width + TRACK_W, :width],
    )


def solution(mesh):
    return jax.shard_map(
        functools.partial(local, mesh.shape["seq"]),
        mesh=mesh,
        in_specs=(P("seq", None), P(), P(), P(), P(), P("seq", None)),
        out_specs=(P("seq", None), P("seq", None), P(), P(), P(), P()),
        check_vma=False,
    )
```

```python
import functools

import jax
import jax.numpy as jnp
from jax import lax
from jax.experimental import pallas as pl
from jax.experimental.pallas import tpu as pltpu
from jax.sharding import PartitionSpec as P

TRACK_W = 16
LANES = 128
TILE = 512
MESH = pl.DeviceIdType.MESH


def plan(n, rows, width):
    tracks = width // TRACK_W
    total = rows * n
    shifts = [0] + [min(2 ** (t - 1), total // 2) for t in range(1, tracks)]
    near = [t for t in range(1, tracks) if shifts[t] < rows]
    small = [t for t in near if shifts[t] <= LANES]
    groups = []
    for t in range(1, tracks):
        if shifts[t] >= rows:
            hops = (shifts[t] // rows) % n
            if groups and groups[-1][0] == hops:
                groups[-1][2] = t + 1
            else:
                groups.append([hops, t, t + 1])
    return shifts, near, small, groups


def channels(first, last):
    return pl.ds(first * TRACK_W, (last - first) * TRACK_W)


def radices(n):
    factors = []
    for factor in [2] + [4] * 16 + [2] * 2:
        if n % factor == 0 and n > 1:
            factors.append(factor)
            n //= factor
    if n > 1:
        factors.append(n)
    return factors


class Rotation:
    def __init__(self, me, n, sign, src, dst, halo, send, recv):
        self.sign, self.src, self.dst, self.halo = sign, src, dst, halo
        width, rows = src.shape
        self.rows = rows
        self.shifts, self.near, self.small, self.groups = plan(n, rows, width)
        self.copies = []

        def add(source, target, hops):
            k = len(self.copies)
            self.copies.append(
                pltpu.make_async_remote_copy(
                    src_ref=source,
                    dst_ref=target,
                    send_sem=send.at[k],
                    recv_sem=recv.at[k],
                    device_id=(lax.rem(me + (sign * hops) % n, n),),
                    device_id_type=MESH,
                )
            )

        for hops, first, last in sorted(self.groups, reverse=True):
            piece = channels(first, last)
            add(src.at[piece, :], dst.at[piece, :], hops)
        wide = [t for t in self.near if t not in self.small]
        for first, last, size in [(t, t + 1, self.shifts[t]) for t in reversed(wide)] + [
            (self.small[0], self.small[-1] + 1, LANES)
        ]:
            start = rows - size if sign > 0 else 0
            piece = channels(first, last)
            add(src.at[piece, pl.ds(start, size)], halo.at[piece, pl.ds(0, size)], 1)

    def start(self):
        for copy in self.copies:
            copy.start()

    def finish(self):
        rows, src, dst, halo = self.rows, self.src, self.dst, self.halo
        for copy in self.copies:
            copy.wait()
        dst[channels(0, 1), :] = src[channels(0, 1), :]
        lane = lax.broadcasted_iota(jnp.int32, (TRACK_W, LANES), 1)
        for t in self.near:
            s, piece = self.shifts[t], channels(t, t + 1)
            if s % LANES == 0:
                if self.sign > 0:
                    dst[piece, pl.ds(s, rows - s)] = src[piece, pl.ds(0, rows - s)]
                    dst[piece, pl.ds(0, s)] = halo[piece, pl.ds(0, s)]
                else:
                    dst[piece, pl.ds(0, rows - s)] = src[piece, pl.ds(s, rows - s)]
                    dst[piece, pl.ds(rows - s, s)] = halo[piece, pl.ds(0, s)]
                continue
            body = src[piece, :].astype(jnp.float32)
            edge = halo[piece, pl.ds(0, LANES)].astype(jnp.float32)
            if self.sign > 0:
                body = pltpu.roll(body, s, 1)
                edge = pltpu.roll(edge, s, 1)
                first = jnp.where(lane < s, edge, body[:, :LANES])
                body = jnp.concatenate([first, body[:, LANES:]], axis=1)
            else:
                body = pltpu.roll(body, rows - s, 1)
                edge = pltpu.roll(edge, LANES - s, 1)
                last = jnp.where(lane >= LANES - s, edge, body[:, rows - LANES :])
                body = jnp.concatenate([body[:, : rows - LANES], last], axis=1)
            dst[piece, :] = body.astype(jnp.bfloat16)


def dot(a, b):
    return jnp.dot(a, b, preferred_element_type=jnp.float32)


def dot_t(a, b):
    return lax.dot_general(a, b, (((1,), (1,)), ((), ())), preferred_element_type=jnp.float32)


def gelu_both(t):
    c = 0.7978845608028654
    sq = t * t
    th = jnp.tanh(c * (t + 0.044715 * (sq * t)))
    half = 0.5 * (1.0 + th)
    slope = half + (0.5 * t) * ((1.0 - th * th) * (c + (3.0 * 0.044715 * c) * sq))
    return half * t, slope


def kernel(
    n, scale, u0, cot, w_in, w_out_t, b_in_row, b_out_row,
    result, grad, reduced,
    back1, u1, r1, back0, w_in_t, w_out, b_in, b_out,
    halo, act, slope, delta, acc, part, land, own, fin,
    rot_send, rot_recv, rs_send, rs_recv, ag_send, ag_recv,
):
    me = lax.axis_index("seq")
    m0, m1, g1 = result, result, grad
    width, rows = u0.shape
    layers, hidden, _ = w_in_t.shape
    chunk = part.shape[2]
    tile = min(TILE, rows)
    steps = rows // tile

    barrier = pltpu.get_barrier_semaphore()

    def greet(k, carry):
        pl.semaphore_signal(
            barrier, inc=1, device_id=(lax.rem(me + k, n),), device_id_type=MESH
        )
        return carry

    lax.fori_loop(1, n, greet, 0)
    pl.semaphore_wait(barrier, n - 1)

    def rotation(i, sign, src, dst):
        return Rotation(me, n, sign, src, dst, halo.at[i], rot_send.at[i], rot_recv.at[i])

    rot_cot = rotation(0, -1, cot, back1)
    rot_m0 = rotation(1, 1, m0, u1)
    rot_m1 = rotation(2, 1, m1, r1)
    rot_g1 = rotation(3, -1, g1, back0)

    def tiles(body):
        def step(i, carry):
            body(pl.ds(pl.multiple_of(i * tile, tile), tile))
            return carry

        lax.fori_loop(0, steps, step, 0)

    def forward(l, u, out):
        def body(cols):
            x = u[:, cols]
            pre = dot(w_in_t[l], x) + b_in[l]
            a, d = gelu_both(pre)
            a = a.astype(jnp.bfloat16)
            act[l, :, cols] = a
            slope[l, :, cols] = d
            out[:, cols] = (x.astype(jnp.float32) + dot(w_out_t[l], a) + b_out[l]).astype(
                jnp.bfloat16
            )

        tiles(body)

    def backward(l, back, out):
        def body(cols):
            b = back[:, cols]
            d = (dot(w_out[l], b) * slope[l, :, cols]).astype(jnp.bfloat16)
            delta[:, cols] = d
            out[:, cols] = (b.astype(jnp.float32) + dot(w_in[l], d)).astype(jnp.bfloat16)

        tiles(body)

    def weight_grads(l, u, back):
        ones = jnp.ones((TRACK_W, tile), jnp.bfloat16)

        def body(cols):
            b, d = back[:, cols], delta[:, cols]
            acc[l, pl.ds(0, width), :] += dot_t(b, act[l, :, cols])
            acc[l, pl.ds(width, width + TRACK_W), :] += dot_t(
                jnp.concatenate([u[:, cols], ones], axis=0), d
            )
            acc[l, pl.ds(2 * width + TRACK_W, 8), pl.ds(0, width)] += dot_t(ones, b)[:8]

        tiles(body)

    stages, stride, length, first, offset = [], 1, n, 0, 0
    for radix in radices(n):
        digit = lax.rem(me // stride, radix)
        share = length // radix
        mine = first + digit * share
        stages.append((radix, stride, digit, share, first, mine, offset))
        first, length, stride, offset = mine, share, stride * radix, offset + (radix - 1) * share
    last = len(stages) - 1

    def rows_of(i):
        return pl.ds(pl.multiple_of(i * chunk, 8), chunk)

    def exchange(s, j, src, dst, sends, recvs):
        radix, stride, digit = stages[s][:3]
        return pltpu.make_async_remote_copy(
            src_ref=src,
            dst_ref=dst,
            send_sem=sends.at[s, j],
            recv_sem=recvs.at[s, j],
            device_id=(me + (lax.rem(digit + j, radix) - digit) * stride,),
            device_id_type=MESH,
        )

    def scatter(l, s):
        radix, _, digit, share, first, _, offset = stages[s]
        return [
            exchange(
                s, j,
                part.at[l, pl.ds(first + lax.rem(digit + j, radix) * share, share)],
                land.at[l, pl.ds(offset + (j - 1) * share, share)],
                rs_send.at[l], rs_recv.at[l],
            )
            for j in range(1, radix)
        ]

    def gather(l, s, arriving):
        radix, _, digit, share, first, mine, _ = stages[s]
        return [
            exchange(
                s, j,
                fin.at[l, pl.ds(mine, share)],
                fin.at[
                    l,
                    pl.ds(first + lax.rem(digit + radix - j, radix) * share, share)
                    if arriving
                    else pl.ds(mine, share),
                ],
                ag_send.at[l], ag_recv.at[l],
            )
            for j in range(1, radix)
        ]

    def scatter_start(l):
        def narrow(i, carry):
            part[l, i] = acc[l, rows_of(i), :].astype(jnp.bfloat16)
            return carry

        lax.fori_loop(0, n, narrow, 0)
        for copy in scatter(l, 0):
            copy.start()

    def scatter_step(l, s):
        radix, _, _, share, _, mine, offset = stages[s]
        for copy in scatter(l, s):
            copy.wait()

        def add(i, carry):
            total = acc[l, rows_of(mine + i), :]
            for j in range(radix - 1):
                total = total + land[l, offset + j * share + i].astype(jnp.float32)
            if s < last:
                acc[l, rows_of(mine + i), :] = total
                part[l, mine + i] = total.astype(jnp.bfloat16)
            else:
                fin[l, mine + i] = (total * scale).astype(jnp.bfloat16)
            return carry

        lax.fori_loop(0, share, add, 0)
        for copy in scatter(l, s + 1) if s < last else gather(l, last, False):
            copy.start()

    def gather_step(l, s):
        for copy in gather(l, s, True):
            copy.wait()
        if s > 0:
            for copy in gather(l, s - 1, False):
                copy.start()

    rot_cot.start()
    w_in_t[0] = w_in[0].T
    for l in range(layers):
        for row, column in ((b_in_row, b_in), (b_out_row, b_out)):
            spread = jnp.broadcast_to(row[l : l + 1, :], (LANES, row.shape[1]))
            column[l] = spread.T[:, :1]
    forward(0, u0, m0)
    rot_m0.start()
    for l in range(1, layers):
        w_in_t[l] = w_in[l].T
    for l in range(layers):
        w_out[l] = w_out_t[l].T
    acc[...] = jnp.zeros_like(acc)
    rot_cot.finish()
    rot_m0.finish()
    forward(1, u1, m1)
    backward(1, back1, g1)
    rot_g1.start()
    weight_grads(1, u1, back1)
    scatter_start(1)
    rot_g1.finish()
    rot_m1.start()
    backward(0, back0, grad)
    todo = [functools.partial(scatter_step, s=s) for s in range(last + 1)]
    todo += [functools.partial(gather_step, s=s) for s in reversed(range(last + 1))]
    todo[0](1)
    weight_grads(0, u0, back0)
    scatter_start(0)
    todo[1](1)
    rot_m1.finish()
    result[...] = r1[...]
    for step in range(len(todo)):
        todo[step](0)
        if step + 2 < len(todo):
            todo[step + 2](1)
    reduced[...] = fin[...]


def local(n, tokens, w_in, b_in, w_out, b_out, cotangent):
    rows, width = tokens.shape
    layers, _, hidden = w_in.shape
    scale = 1.0 / (rows * n) ** 0.5
    needed = 2 * width + TRACK_W + 8
    chunk = -(-needed // (8 * n)) * 8
    shifts, near, small, groups = plan(n, rows, width)
    factors = radices(n)
    copies = len(groups) + len(near) - len(small) + 1
    bf16, f32 = jnp.bfloat16, jnp.float32
    vmem = pl.BlockSpec(memory_space=pltpu.VMEM)
    block = pltpu.VMEM((width, rows), bf16)
    result, grad, reduced = pl.pallas_call(
        functools.partial(kernel, n, scale),
        out_shape=[
            jax.ShapeDtypeStruct((width, rows), bf16),
            jax.ShapeDtypeStruct((width, rows), bf16),
            jax.ShapeDtypeStruct((layers, n, chunk, hidden), bf16),
        ],
        in_specs=[vmem] * 6,
        out_specs=[vmem] * 3,
        scratch_shapes=[block] * 4
        + [
            pltpu.VMEM((layers, hidden, width), bf16),
            pltpu.VMEM((layers, hidden, width), bf16),
            pltpu.VMEM((layers, hidden, 1), f32),
            pltpu.VMEM((layers, width, 1), f32),
            pltpu.VMEM((4, (near[-1] + 1) * TRACK_W, rows // 2), bf16),
            pltpu.VMEM((layers, hidden, rows), bf16),
            pltpu.VMEM((layers, hidden, rows), f32),
            pltpu.VMEM((hidden, rows), bf16),
            pltpu.VMEM((layers, n * chunk, hidden), f32),
            pltpu.VMEM((layers, n, chunk, hidden), bf16),
            pltpu.VMEM((layers, n, chunk, hidden), bf16),
            pltpu.VMEM((layers, chunk, hidden), bf16),
            pltpu.VMEM((layers, n, chunk, hidden), bf16),
            pltpu.SemaphoreType.DMA((4, copies)),
            pltpu.SemaphoreType.DMA((4, copies)),
        ]
        + [pltpu.SemaphoreType.DMA((layers, len(factors), max(factors)))] * 4,
        compiler_params=pltpu.CompilerParams(
            collective_id=0, has_side_effects=True, vmem_limit_bytes=64 * 1024 * 1024 - 65536
        ),
    )(
        tokens.T,
        cotangent.T,
        w_in,
        w_out.transpose(0, 2, 1),
        b_in,
        b_out,
    )
    sums = reduced.reshape(layers, n * chunk, hidden)
    return (
        result.T,
        grad.T,
        sums[:, width : 2 * width].astype(f32),
        sums[:, 2 * width].astype(f32),
        sums[:, :width].transpose(0, 2, 1).astype(f32),
        sums[:, 2 * width + TRACK_W, :width].astype(f32),
    )


def solution(mesh):
    return jax.shard_map(
        functools.partial(local, mesh.shape["seq"]),
        mesh=mesh,
        in_specs=(P("seq", None), P(), P(), P(), P(), P("seq", None)),
        out_specs=(P("seq", None), P("seq", None), P(), P(), P(), P()),
        check_vma=False,
    )
```
